32 devices in a mesh: dp: 8 (over y, x, core), tensor: 4 (over z).
Axes of the slice: x: 2, y: 2, z: 4, core: 2. Of those that a mesh axis runs over, the one named last changes fastest.
Arguments:
- x_in: bfloat16 [16, 580, 1024], P('dp', 'tensor'), may hold values from -6 to 6
- out_grad: bfloat16 [16, 580, 1024], P('dp', 'tensor'), may hold values from -6 to 6
- ln1_gain: bfloat16 [1024], replicated, may hold values from 0.5 to 1.5
- ln1_shift: bfloat16 [1024], replicated, may hold values from -1.75 to 1.75
- ln2_gain: bfloat16 [1024], replicated, may hold values from 0.5 to 1.5
- ln2_shift: bfloat16 [1024], replicated, may hold values from -1.75 to 1.75
- w_qkv: bfloat16 [1024, 3, 1024], P('dp', None, 'tensor'), may hold values from -0.1875 to 0.1875
- qv_bias: bfloat16 [2, 1024], P(None, 'tensor'), may hold values from -1.75 to 1.75
- w_out: bfloat16 [1024, 1024], P('tensor', 'dp'), may hold values from -0.375 to 0.375
- out_bias: bfloat16 [1024], replicated, may hold values from -1.75 to 1.75
- w_fc1: bfloat16 [1024, 4096], P('dp', 'tensor'), may hold values from -0.1875 to 0.1875
- fc1_bias: bfloat16 [4096], P('tensor'), may hold values from -1.75 to 1.75
- w_fc2: bfloat16 [4096, 1024], P('tensor', 'dp'), may hold values from -0.09375 to 0.09375
- fc2_bias: bfloat16 [1024], replicated, may hold values from -1.75 to 1.75
- a_qkv: bfloat16 [8, 1024, 48], replicated, may hold values from -0.1875 to 0.1875
- b_qkv: bfloat16 [8, 16, 3, 1024], P(None, None, None, 'tensor'), may hold values from -1.5 to 1.5
- a_out: bfloat16 [8, 1024, 16], P(None, 'tensor'), may hold values from -0.1875 to 0.1875
- b_out: bfloat16 [8, 16, 1024], replicated, may hold values from -1.5 to 1.5
- a_fc1: bfloat16 [8, 1024, 16], replicated, may hold values from -0.1875 to 0.1875
- b_fc1: bfloat16 [8, 16, 4096], P(None, None, 'tensor'), may hold values from -1.5 to 1.5
- a_fc2: bfloat16 [8, 4096, 16], P(None, 'tensor'), may hold values from -0.09375 to 0.09375
- b_fc2: bfloat16 [8, 16, 1024], replicated, may hold values from -1.5 to 1.5
- adapter_index: int32 [16], P('dp'), may hold values from 0 to 7
- valid_tokens: int32 [16], P('dp'), may hold values from 144 to 577, as said below
- live_images: int32 [8], P('dp'), may hold values from 1 to 2, as said below
Outputs:
- layer_out: bfloat16 [16, 580, 1024], P('dp', 'tensor')
- x_grad: bfloat16 [16, 580, 1024], P('dp', 'tensor')
- grad_a_qkv: float32 [8, 1024, 48], replicated
- grad_b_qkv: float32 [8, 16, 3, 1024], P(None, None, None, 'tensor')
- grad_a_out: float32 [8, 1024, 16], P(None, 'tensor')
- grad_b_out: float32 [8, 16, 1024], replicated
- grad_a_fc1: float32 [8, 1024, 16], replicated
- grad_b_fc1: float32 [8, 16, 4096], P(None, None, 'tensor')
- grad_a_fc2: float32 [8, 4096, 16], P(None, 'tensor')
- grad_b_fc2: float32 [8, 16, 1024], replicated
The draws below stay inside these ranges and needn't reach their ends.
Inputs may be any that keep to these rules, and one draw needn't show every extreme that they name: `valid_tokens`: keys at positions from an image's count on are padding; some image has exactly 577. `live_images`: image slots of an index of dp at or beyond its count hold no image; some index of dp has all 2 slots filled.
All inputs are finite; a program needn't handle non-finite values.
Results may differ from the reference program's by a relative error of at most 0.023.
The reference program's roundings to bfloat16 on the way count: a program that leaves them out, or rounds other values in their place, can miss the bound.
Values may be sent and summed in bfloat16 or wider, within the bound.
No kernel may reach another device: no remote copies, remote signals or barrier semaphores. Data moves between devices by JAX's collectives and lax.ppermute only.
A program may use at most 128 MiB of HBM per device.

```python
import jax
import jax.numpy as jnp
from jax import lax

D = 1024
HEADS = 16
HD = 64
FF = 4096
SEQ = 580
VALID = 577
ADAPTERS = 8
RANK = 16
SLOTS = 2
GROUPS = 8
IMAGES = 16


def draw_valid_tokens(key, part):
    draw_key, pick_key = jax.random.split(jax.random.fold_in(key, 11))
    lengths = jax.random.randint(draw_key, (IMAGES,), VALID // 4, VALID + 1)
    chosen = jax.random.randint(pick_key, (), 0, IMAGES)
    return jnp.where(jnp.arange(IMAGES) == chosen, VALID, lengths).astype(jnp.int32)


def draw_live_images(key, part):
    draw_key, pick_key = jax.random.split(jax.random.fold_in(key, 23))
    counts = jax.random.randint(draw_key, (GROUPS,), 1, SLOTS + 1)
    chosen = jax.random.randint(pick_key, (), 0, GROUPS)
    return jnp.where(jnp.arange(GROUPS) == chosen, SLOTS, counts).astype(jnp.int32)


def plant(drawn, rng, smallest, largest):
    dims = drawn.shape
    index_at = [jax.random.randint(jax.random.fold_in(rng, axis), (), 0, dims[axis]) for axis in range(len(dims))]
    drawn = drawn.at[tuple(index_at)].set(smallest)
    longest = dims.index(max(dims))
    index_at[longest] = (index_at[longest] + 1) % dims[longest]
    return drawn.at[tuple(index_at)].set(largest)


def steps_of(rng, extent, cuts, smallest, high):
    level, own = 1.0, jax.random.fold_in(rng, 6)
    for position, parts in cuts:
        steps = jnp.exp(jax.random.uniform(jax.random.fold_in(own, position), (parts,), jnp.float32, smallest / len(cuts), high / len(cuts)))
        level = level * jnp.repeat(steps, extent[position] // parts).reshape([-1 if axis == position else 1 for axis in range(len(extent))])
    return level


def normal_values(rng, dims, scale, reach, shards=(), kind=jnp.bfloat16):
    values = jax.random.normal(rng, dims, jnp.float32) * scale
    if len(shards) > 0:
        values = steps_of(rng, dims, shards, -0.22, 0.18) * values
    return jnp.clip(values, min=-reach, max=reach).astype(kind)


def setup_inputs(seed: int = 0) -> dict:
    seeds = jax.random.split(jax.random.key(seed), 26)
    return {
        "x_in": normal_values(seeds[0], (IMAGES, SEQ, D), 1.0, 6.0, ((0, 8), (1, 4))),
        "out_grad": normal_values(seeds[1], (IMAGES, SEQ, D), 1.0, 6.0, ((0, 8), (1, 4))),
        "ln1_gain": jnp.clip(1.0 + 0.1 * jax.random.normal(seeds[2], (D,), jnp.float32), 0.5, 1.5).astype(jnp.bfloat16),
        "ln1_shift": normal_values(seeds[3], (D,), 0.3, 1.75),
        "ln2_gain": jnp.clip(1.0 + 0.1 * jax.random.normal(seeds[4], (D,), jnp.float32), 0.5, 1.5).astype(jnp.bfloat16),
        "ln2_shift": normal_values(seeds[5], (D,), 0.3, 1.75),
        "w_qkv": normal_values(seeds[6], (D, 3, D), D ** -0.5, 0.1875, ((0, 8), (2, 4))),
        "qv_bias": normal_values(seeds[7], (2, D), 0.3, 1.75, ((1, 4),)),
        "w_out": normal_values(seeds[8], (D, D), (D // 4) ** -0.5, 0.375, ((0, 4), (1, 8))),
        "out_bias": normal_values(seeds[9], (D,), 0.3, 1.75),
        "w_fc1": normal_values(seeds[10], (D, FF), D ** -0.5, 0.1875, ((0, 8), (1, 4))),
        "fc1_bias": normal_values(seeds[11], (FF,), 0.3, 1.75, ((0, 4),)),
        "w_fc2": normal_values(seeds[12], (FF, D), FF ** -0.5, 0.09375, ((0, 4), (1, 8))),
        "fc2_bias": normal_values(seeds[13], (D,), 0.3, 1.75),
        "a_qkv": normal_values(seeds[14], (ADAPTERS, D, 3 * RANK), D ** -0.5, 0.1875),
        "b_qkv": normal_values(seeds[15], (ADAPTERS, RANK, 3, D), RANK ** -0.5, 1.5, ((3, 4),)),
        "a_out": normal_values(seeds[16], (ADAPTERS, D, RANK), D ** -0.5, 0.1875, ((1, 4),)),
        "b_out": normal_values(seeds[17], (ADAPTERS, RANK, D), RANK ** -0.5, 1.5),
        "a_fc1": normal_values(seeds[18], (ADAPTERS, D, RANK), D ** -0.5, 0.1875),
        "b_fc1": normal_values(seeds[19], (ADAPTERS, RANK, FF), RANK ** -0.5, 1.5, ((2, 4),)),
        "a_fc2": normal_values(seeds[20], (ADAPTERS, FF, RANK), FF ** -0.5, 0.09375, ((1, 4),)),
        "b_fc2": normal_values(seeds[21], (ADAPTERS, RANK, D), RANK ** -0.5, 1.5),
        "adapter_index": plant(jax.random.randint(seeds[22], (IMAGES,), 0, ADAPTERS), jax.random.fold_in(seeds[22], 1), 0, ADAPTERS - 1).astype(jnp.int32),
        "valid_tokens": draw_valid_tokens(jax.random.fold_in(seeds[25], 71), 0),
        "live_images": draw_live_images(jax.random.fold_in(seeds[25], 71), 0),
    }


@jax.custom_vjp
def low(v):
    return lax.optimization_barrier(v.astype(jnp.bfloat16)).astype(jnp.float32)

@jax.custom_vjp
def low_back(v):
    return v

def low_keep(v):
    return (low(v), None)

def low_pass(kept, grad):
    return (grad,)

def back_keep(v):
    return (v, None)

def back_low(kept, grad):
    return (low(grad),)
low.defvjp(low_keep, low_pass)
low_back.defvjp(back_keep, back_low)

def product(pattern, left_arg, right_arg):
    return jnp.einsum(pattern, left_arg, right_arg, precision=lax.Precision.HIGHEST)

def normalize(values, gain, shift):
    average = lax.optimization_barrier(jnp.mean(values, axis=-1, keepdims=True))
    centred = values - average
    spread = lax.optimization_barrier(jnp.mean(centred * centred, axis=-1, keepdims=True))
    return centred * lax.rsqrt(spread + 1e-05) * gain + shift

def forward(field, adjusted, frozen, picks, valid, live_mask):
    a_qkv, b_qkv, a_out, b_out, a_fc1, b_fc1, a_fc2, b_fc2 = adjusted
    ln1_gain, ln1_shift, ln2_gain, ln2_shift, w_qkv, qv_bias, w_out, out_bias, w_fc1, fc1_bias, w_fc2, fc2_bias = frozen
    image_count = field.shape[0]
    seq_length = field.shape[1]
    model_width = field.shape[2]
    low_rank = a_out.shape[2]
    first_norm = low(normalize(field, ln1_gain, ln1_shift))
    adapter_qkv = low(low_back(product('bsd,bdr->bsr', first_norm, a_qkv[picks])))
    adapter_qkv = adapter_qkv.reshape(image_count, seq_length, 3, low_rank)
    qkv_bias = jnp.stack([qv_bias[0], jnp.zeros_like(qv_bias[0]), qv_bias[1]])
    projected = product('bsd,dkc->bskc', first_norm, w_qkv) + qkv_bias + product('bskr,brkc->bskc', adapter_qkv, b_qkv[picks])
    projected = low(low_back(projected))
    head_rows = projected.reshape(image_count, seq_length, 3, HEADS, HD)
    query_rows = head_rows[:, :, 0]
    key_rows = head_rows[:, :, 1]
    value_rows = head_rows[:, :, 2]
    scores = low_back(product('bqhe,bkhe->bhqk', query_rows, key_rows) * HD ** (-0.5))
    key_mask = jnp.arange(seq_length)[None, :] < valid[:, None]
    scores = jnp.where(key_mask[:, None, None, :], scores, -1000000000.0)
    attn_probs = low(jax.nn.softmax(scores, axis=-1))
    attended = product('bhqk,bkhe->bqhe', attn_probs, value_rows).reshape(image_count, seq_length, model_width)
    attended = low(low_back(attended))
    adapter_out = low(low_back(product('bsd,bdr->bsr', attended, a_out[picks])))
    branch = product('bsd,dc->bsc', attended, w_out) + out_bias + product('bsr,brc->bsc', adapter_out, b_out[picks])
    resid = field + low_back(branch)
    second_norm = low(normalize(resid, ln2_gain, ln2_shift))
    adapter_fc1 = low(low_back(product('bsd,bdr->bsr', second_norm, a_fc1[picks])))
    pre_act = product('bsd,df->bsf', second_norm, w_fc1) + fc1_bias + product('bsr,brf->bsf', adapter_fc1, b_fc1[picks])
    pre_act = low_back(pre_act)
    hidden = low(pre_act * jax.nn.sigmoid(1.702 * pre_act))
    adapter_fc2 = low(low_back(product('bsf,bfr->bsr', hidden, a_fc2[picks])))
    second = product('bsf,fc->bsc', hidden, w_fc2) + fc2_bias + product('bsr,brc->bsc', adapter_fc2, b_fc2[picks])
    return (resid + low_back(second)) * live_mask[:, None, None]

def reference(x_in, out_grad, ln1_gain, ln1_shift, ln2_gain, ln2_shift, w_qkv, qv_bias, w_out, out_bias, w_fc1, fc1_bias, w_fc2, fc2_bias, a_qkv, b_qkv, a_out, b_out, a_fc1, b_fc1, a_fc2, b_fc2, adapter_index, valid_tokens, live_images):
    frozen = tuple((item.astype(jnp.float32) for item in (ln1_gain, ln1_shift, ln2_gain, ln2_shift, w_qkv, qv_bias, w_out, out_bias, w_fc1, fc1_bias, w_fc2, fc2_bias)))
    adjusted = tuple((item.astype(jnp.float32) for item in (a_qkv, b_qkv, a_out, b_out, a_fc1, b_fc1, a_fc2, b_fc2)))
    group_count = live_images.shape[0]
    fields = x_in.astype(jnp.float32).reshape(group_count, SLOTS, SEQ, D)
    cotangents = out_grad.astype(jnp.float32).reshape(group_count, SLOTS, SEQ, D)
    picks = adapter_index.reshape(group_count, SLOTS)
    valid = valid_tokens.reshape(group_count, SLOTS)
    live_mask = (jnp.arange(SLOTS)[None, :] < live_images[:, None]).astype(jnp.float32)
    totals = jax.tree.map(jnp.zeros_like, adjusted)

    def group_step(carried, batch):
        field_group, cot_group, pick_group, valid_group, live_group = batch
        result, pullback = jax.vjp(lambda field, adapters: forward(field, adapters, frozen, pick_group, valid_group, live_group), field_group, adjusted)
        field_grad, adjusted_grad = pullback(cot_group)
        carried = jax.tree.map(lambda left_arg, right_arg: left_arg + right_arg, carried, adjusted_grad)
        return (carried, (result.astype(jnp.bfloat16), field_grad.astype(jnp.bfloat16)))
    totals, (results, field_grads) = lax.scan(group_step, totals, (fields, cotangents, picks, valid, live_mask))
    layer_out = results.reshape(IMAGES, SEQ, D)
    x_grad = field_grads.reshape(IMAGES, SEQ, D)
    return (layer_out, x_grad, totals[0], totals[1], totals[2], totals[3], totals[4], totals[5], totals[6], totals[7])
```

```python
import functools

import jax
import jax.numpy as jnp
import numpy as np
from jax import lax
from jax.experimental import pallas as pl
from jax.experimental.pallas import tpu as pltpu
from jax.sharding import Mesh, PartitionSpec as P

HD = 64
LANE = 128
F32 = jnp.float32
BF16 = jnp.bfloat16
NEG = -1000000000.0

AD, LEN, LIVE, CORE, ZPOS = 0, 1, 2, 3, 4
IDX, TMAP, QPOS = 8, 16, 20


def dot(left, right, lc=1, rc=0):
    return lax.dot_general(left, right, (((lc,), (rc,)), ((), ())), preferred_element_type=F32)


def lanes(pieces):
    return jnp.concatenate(pieces, axis=1)


def rows_of(pieces):
    return jnp.concatenate(pieces, axis=0)


def widen(block, count):
    return rows_of([block, jnp.zeros((count - block.shape[0], block.shape[1]), block.dtype)])


def full(shape):
    return pl.BlockSpec(shape, lambda *a: (0,) * len(shape))


def call(kernel, sc, operands, in_specs, out_specs, out_shape, grid, scratch=(), name=None, cost=None):
    flops, bytes_accessed = cost if cost is not None else (1 << 30, 1 << 22)
    return pl.pallas_call(
        kernel,
        out_shape=out_shape,
        grid_spec=pltpu.PrefetchScalarGridSpec(
            num_scalar_prefetch=1,
            grid=grid,
            in_specs=in_specs,
            out_specs=out_specs,
            scratch_shapes=list(scratch),
        ),
        compiler_params=pltpu.CompilerParams(vmem_limit_bytes=44 << 20),
        cost_estimate=pl.CostEstimate(flops=flops, bytes_accessed=bytes_accessed, transcendentals=0),
        name=name,
    )(sc, *operands)


def center(values):
    average = jnp.mean(values, axis=-1, keepdims=True)
    centred = values - average
    spread = jnp.mean(centred * centred, axis=-1, keepdims=True)
    scale = lax.rsqrt(spread + 1e-05)
    return centred * scale, scale


def enter_kernel(chunks, sc, xa, xb, xc, xd, gain, shift, down, x_out, n_out, u_out):
    wide = widen(down[0], LANE)
    gain_wide = gain[...].astype(F32)
    shift_wide = shift[...].astype(F32)
    rows = xa.shape[0]
    for at, ref in enumerate((xa, xb, xc, xd)):
        start = pl.multiple_of(sc[QPOS + at] * rows, 32)
        value = ref[...]
        hat, _ = center(value.astype(F32))
        norm = (hat * gain_wide + shift_wide).astype(BF16)
        for i in range(chunks):
            x_out[i, pl.ds(start, rows), :] = value[:, i * LANE : (i + 1) * LANE]
            n_out[i, pl.ds(start, rows), :] = norm[:, i * LANE : (i + 1) * LANE]
        u_out[pl.ds(start, rows), :] = dot(norm, wide, 1, 1).astype(BF16)


def pick_diagonal(step, first, second, held):
    @pl.when(step == 0)
    def _():
        held[...] = first[...]

    @pl.when(step == 1)
    def _():
        held[...] = second[...]


def tiles(parts, k, at):
    return [parts[j][0, k, n] for j in range(4) for n in at] if False else None


def order(sc):
    return [sc[IDX + i] for i in range(8)]


def key_rows_valid(sc, total, quarter, used):
    at = lax.broadcasted_iota(jnp.int32, (total, 1), 0)
    block = sum((at >= n * quarter).astype(jnp.int32) for n in range(1, 4))
    inner = at - block * quarter
    return (inner < used) & (block * used + inner < sc[LEN])


def spans(total):
    out, at = [], 0
    while at < total:
        width = min(256, total - at)
        out.append((at, width))
        at += width
    return out


def attend_kernel(
    used, last, sc, n_in, u_in, w0, w1, w2, da, db, up, bias, down, *rest
):
    if last:
        acc_in, qkv_out, o_out, lse_out, out_ref, held, acc = rest
    else:
        qkv_out, o_out, lse_out, out_ref, held, acc = rest
    step = pl.program_id(0)
    total = n_in.shape[1]
    pick_diagonal(step, da, db, held)
    parts = (w0, w1, w2, held)
    at = order(sc)
    norm = lanes([n_in[i] for i in at])
    mats = rows_of([lanes([parts[j][0, k, n] for n in range(3)]) for j in range(4) for k in range(2)])
    zero = jnp.zeros((up.shape[2], LANE), BF16)
    adapt = widen(rows_of([lanes([up[0, j] if i == j else zero for i in range(3)]) for j in range(3)]), LANE)
    bias_row = lanes([bias[0, 0:1, :], jnp.zeros((1, LANE), BF16), bias[0, 1:2, :]]).astype(F32)
    result = (dot(norm, mats) + bias_row + dot(u_in[...], adapt)).astype(BF16)
    for j in range(3):
        qkv_out[0, j] = result[:, j * LANE : (j + 1) * LANE]
    query = result[:, :LANE] * jnp.asarray(HD ** (-0.5), BF16)
    key = result[:, LANE : 2 * LANE]
    value = result[:, 2 * LANE :]
    lane = lax.broadcasted_iota(jnp.int32, (1, LANE), 1)
    valid = key_rows_valid(sc, total, total // 4, used)
    heads = [jnp.where((lane >= h * HD) & (lane < (h + 1) * HD), key, jnp.zeros_like(key)) for h in range(2)]
    for start, width in spans(total):
        block = query[start : start + width]
        pieces = []
        for h in range(2):
            scores = jnp.where(valid, dot(heads[h], block, 1, 1), NEG)
            top = jnp.max(scores, axis=0, keepdims=True)
            shifted = jnp.exp(scores - top)
            total_row = jnp.sum(shifted, axis=0, keepdims=True)
            mixed = dot(value, shifted.astype(BF16), 0, 0)
            pieces.append(mixed[h * HD : (h + 1) * HD] / total_row)
            lse_out[0, h : h + 1, start : start + width] = top + jnp.log(total_row)
        o_out[0, start : start + width, :] = rows_of(pieces).T.astype(BF16)
    attended = o_out[0]
    outs = lanes([parts[j][0, k, 3] for j in range(4) for k in range(2)])
    branch = dot(attended, outs)
    small = dot(attended, widen(down[0], LANE), 1, 1)

    @pl.when(step == 0)
    def _():
        if last:
            acc[:, :1024] = acc_in[:, :1024] + branch
            acc[:, 1024:] = acc_in[:, 1024:] + small
        else:
            acc[:, :1024] = branch
            acc[:, 1024:] = small

    @pl.when(step == 1)
    def _():
        if last:
            for i in range(8):
                out_ref[at[i]] = (acc[:, i * LANE : (i + 1) * LANE] + branch[:, i * LANE : (i + 1) * LANE]).astype(BF16)
            out_ref[8] = (acc[:, 1024:] + small).astype(BF16)
        else:
            out_ref[:, :1024] = acc[:, :1024] + branch
            out_ref[:, 1024:] = acc[:, 1024:] + small


def middle_kernel(sc, own, other, x_in, bias, up, gain, shift, down, resid_out, n_out, u_out, uo_out):
    rows = own.shape[1]
    small = (own[8].astype(F32) + other[8].astype(F32)).astype(BF16)
    uo_out[...] = small
    added = dot(small, widen(up[0], LANE)) + bias[...].astype(F32)
    branch = lanes([own[i].astype(F32) + other[i].astype(F32) for i in range(8)]) + added
    resid = lanes([x_in[i] for i in range(8)]).astype(F32) + branch
    hat, _ = center(resid)
    norm = (hat * gain[...].astype(F32) + shift[...].astype(F32)).astype(BF16)
    for i in range(8):
        resid_out[i] = resid[:, i * LANE : (i + 1) * LANE]
        n_out[i] = norm[:, i * LANE : (i + 1) * LANE]
    u_out[...] = dot(norm, widen(down[0], LANE), 1, 1).astype(BF16)


def cotangent_kernel(sc, ga, gb, gc, gd, up, d_out, du_out):
    rows = ga.shape[0]
    wide = widen(up[0], LANE)
    keep = (sc[LIVE] > 0).astype(F32)
    for at, ref in enumerate((ga, gb, gc, gd)):
        start = pl.multiple_of(sc[QPOS + at] * rows, 32)
        value = (ref[...].astype(F32) * keep).astype(BF16)
        for i in range(8):
            d_out[i, pl.ds(start, rows), :] = value[:, i * LANE : (i + 1) * LANE]
        du_out[pl.ds(start, rows), :] = dot(value, wide, 1, 1).astype(BF16)


def feed_kernel(last, sc, n_in, u_in, d_in, du_in, w0, w1, w2, da, db, up, down, bias, *rest):
    if last:
        y_in, dn_in, y_out, dn_out, gup_out, gdown_out, held, y_acc, dn_acc, g_keep, df_keep = rest
    else:
        y_out, dn_out, gup_out, gdown_out, held, y_acc, dn_acc, g_keep, df_keep = rest
    step = pl.program_id(0)
    pick_diagonal(step, da, db, held)
    parts = (w0, w1, w2, held)
    at = order(sc)
    norm = lanes([n_in[i] for i in at])
    cot = lanes([d_in[i] for i in at])
    u1 = u_in[...]
    du2 = du_in[...]
    jk = [(j, k) for j in range(4) for k in range(2)]
    for half in range(2):
        pair = (2 * half, 2 * half + 1)
        up_mat = rows_of([lanes([parts[j][0, k, n] for n in pair]) for j, k in jk])
        down_mat = rows_of([lanes([parts[j][0, k, 4 + n] for j, k in jk]) for n in pair])
        up_small = widen(lanes([up[0, n] for n in pair]), LANE)
        down_small = widen(lanes([down[0, n] for n in pair]), LANE)
        bias_row = lanes([bias[0, n : n + 1, :] for n in pair]).astype(F32)
        pre = dot(norm, up_mat) + bias_row + dot(u1, up_small)
        squash = jax.nn.sigmoid(1.702 * pre)
        hidden = (pre * squash).astype(BF16)
        grad = dot(cot, down_mat, 1, 1) + dot(du2, down_small)
        dpre = (grad * (squash + 1.702 * pre * squash * (1.0 - squash))).astype(BF16)
        g_keep[:, half * 256 : (half + 1) * 256] = hidden
        df_keep[:, half * 256 : (half + 1) * 256] = dpre
    hidden = g_keep[...]
    dpre = df_keep[...]
    up_mat = rows_of([lanes([parts[j][0, k, n] for n in range(4)]) for j, k in jk])
    down_mat = rows_of([lanes([parts[j][0, k, 4 + n] for j, k in jk]) for n in range(4)])
    up_small = widen(lanes([up[0, n] for n in range(4)]), LANE)
    down_small = widen(lanes([down[0, n] for n in range(4)]), LANE)
    y_part = dot(hidden, down_mat)
    y_small = dot(hidden, down_small, 1, 1)
    dn_part = dot(dpre, up_mat, 1, 1)
    dn_small = dot(dpre, up_small, 1, 1)
    gup = dot(u1, dpre, 0, 0)
    gdown = dot(du2, hidden, 0, 0)
    for n in range(4):
        gup_out[0, n] = gup[: up.shape[2], n * LANE : (n + 1) * LANE].astype(BF16)
        gdown_out[0, n] = gdown[: up.shape[2], n * LANE : (n + 1) * LANE].astype(BF16)

    @pl.when(step == 0)
    def _():
        if last:
            y_acc[:, :1024] = y_in[:, :1024] + y_part
            y_acc[:, 1024:] = y_in[:, 1024:] + y_small
            dn_acc[:, :1024] = dn_in[:, :1024] + dn_part
            dn_acc[:, 1024:] = dn_in[:, 1024:] + dn_small
        else:
            y_acc[:, :1024] = y_part
            y_acc[:, 1024:] = y_small
            dn_acc[:, :1024] = dn_part
            dn_acc[:, 1024:] = dn_small

    @pl.when(step == 1)
    def _():
        if last:
            for i in range(8):
                cut = slice(i * LANE, (i + 1) * LANE)
                y_out[at[i]] = (y_acc[:, cut] + y_part[:, cut]).astype(BF16)
                dn_out[at[i]] = (dn_acc[:, cut] + dn_part[:, cut]).astype(BF16)
            y_out[8] = (y_acc[:, 1024:] + y_small).astype(BF16)
            dn_out[8] = (dn_acc[:, 1024:] + dn_small).astype(BF16)
        else:
            y_out[:, :1024] = y_acc[:, :1024] + y_part
            y_out[:, 1024:] = y_acc[:, 1024:] + y_small
            dn_out[:, :1024] = dn_acc[:, :1024] + dn_part
            dn_out[:, 1024:] = dn_acc[:, 1024:] + dn_small


def leave_kernel(sc, own, other, resid, bias, up, d_in, out_ref, gup_out):
    step = pl.program_id(0)
    small = (own[8].astype(F32) + other[8].astype(F32)).astype(BF16)
    added = dot(small, widen(up[0], LANE)) + bias[...].astype(F32)
    second = lanes([own[i].astype(F32) + other[i].astype(F32) for i in range(8)]) + added
    keep = (sc[LIVE] > 0).astype(F32)
    out_ref[...] = ((lanes([resid[i] for i in range(8)]) + second) * keep).astype(BF16)
    grad = dot(small, lanes([d_in[i] for i in range(8)]), 0, 0)[: up.shape[1]]

    @pl.when(step == 0)
    def _():
        gup_out[...] = grad

    @pl.when(step != 0)
    def _():
        gup_out[...] += grad


def middle_back_kernel(sc, own, other, resid, d_in, n_in, uo_in, gain, down, up, dres_out, dz_out, duo_out, gdown_out, gup_out):
    step = pl.program_id(0)
    small = (own[8].astype(F32) + other[8].astype(F32)).astype(BF16)
    dnorm = lanes([own[i].astype(F32) + other[i].astype(F32) for i in range(8)]) + dot(small, widen(down[0], LANE))
    hat, scale = center(lanes([resid[i] for i in range(8)]))
    weighted = dnorm * gain[...].astype(F32)
    first = jnp.mean(weighted, axis=-1, keepdims=True)
    second = jnp.mean(weighted * hat, axis=-1, keepdims=True)
    dres = lanes([d_in[i] for i in range(8)]).astype(F32) + scale * (weighted - first - hat * second)
    dz = dres.astype(BF16)
    for i in range(8):
        dres_out[i] = dres[:, i * LANE : (i + 1) * LANE]
        dz_out[i] = dz[:, i * LANE : (i + 1) * LANE]
    duo_out[...] = dot(dz, widen(up[0], LANE), 1, 1).astype(BF16)
    rank = up.shape[1]
    gdown = dot(small, lanes([n_in[i] for i in range(8)]), 0, 0)[:rank]
    gup = dot(uo_in[...], dz, 0, 0)[:rank]

    @pl.when(step == 0)
    def _():
        gdown_out[...] = gdown
        gup_out[...] = gup

    @pl.when(step != 0)
    def _():
        gdown_out[...] += gdown
        gup_out[...] += gup


def attend_back_kernel(
    used, last, sc, dz_in, duo_in, uq_in, qkv_in, o_in, lse_in, w0, w1, w2, da, db, up, down, *rest
):
    if last:
        acc_in, out_ref, gup_out, gdown_out, held, acc, dq_keep = rest
    else:
        out_ref, gup_out, gdown_out, held, acc, dq_keep = rest
    step = pl.program_id(0)
    total = dz_in.shape[1]
    rank = up.shape[2]
    pick_diagonal(step, da, db, held)
    parts = (w0, w1, w2, held)
    at = order(sc)
    jk = [(j, k) for j in range(4) for k in range(2)]
    dz = lanes([dz_in[i] for i in at])
    outs = lanes([parts[j][0, k, 3] for j, k in jk])
    duo = duo_in[...]
    dattended = (dot(dz, outs, 1, 1) + dot(duo, widen(down[0], LANE))).astype(BF16)
    gdown_out[0] = dot(duo, o_in[0], 0, 0)[:rank].astype(BF16)
    query = qkv_in[0, 0] * jnp.asarray(HD ** (-0.5), BF16)
    key = qkv_in[0, 1]
    value = qkv_in[0, 2]
    lane = lax.broadcasted_iota(jnp.int32, (1, LANE), 1)
    valid = key_rows_valid(sc, total, total // 4, used)
    inside = [(lane >= h * HD) & (lane < (h + 1) * HD) for h in range(2)]
    keys = [jnp.where(inside[h], key, jnp.zeros_like(key)) for h in range(2)]
    values = [jnp.where(inside[h], value, jnp.zeros_like(value)) for h in range(2)]
    dkey = [jnp.zeros((total, LANE), F32) for _ in range(2)]
    dvalue = [jnp.zeros((total, LANE), F32) for _ in range(2)]
    for start, width in spans(total):
        block = query[start : start + width]
        dblock = dattended[start : start + width]
        pieces = []
        for h in range(2):
            scores = dot(keys[h], block, 1, 1)
            probs = jnp.where(valid, jnp.exp(scores - lse_in[0, h : h + 1, start : start + width]), 0.0)
            dprobs = dot(values[h], dblock, 1, 1)
            inner = jnp.sum(probs * dprobs, axis=0, keepdims=True)
            dscores = (probs * (dprobs - inner)).astype(BF16)
            dvalue[h] += dot(probs.astype(BF16), dblock)
            dkey[h] += dot(dscores, block)
            pieces.append(dot(key, dscores, 0, 0)[h * HD : (h + 1) * HD] * (HD ** (-0.5)))
        dq_keep[start : start + width, :] = rows_of(pieces).T.astype(BF16)
    dquery = dq_keep[...]
    dkey_all = jnp.where(inside[0], dkey[0], dkey[1]).astype(BF16)
    dvalue_all = jnp.where(inside[0], dvalue[0], dvalue[1]).astype(BF16)
    grads = lanes([dquery, dkey_all, dvalue_all])
    zero = jnp.zeros((rank, LANE), BF16)
    adapt = widen(rows_of([lanes([up[0, j] if i == j else zero for i in range(3)]) for j in range(3)]), LANE)
    gup = dot(uq_in[...], grads, 0, 0)
    for j in range(3):
        gup_out[0, j] = gup[j * rank : (j + 1) * rank, j * LANE : (j + 1) * LANE].astype(BF16)
    mats = rows_of([lanes([parts[j][0, k, n] for n in range(3)]) for j, k in jk])
    part = dot(grads, mats, 1, 1)
    small = dot(grads, adapt, 1, 1)

    @pl.when(step == 0)
    def _():
        if last:
            acc[:, :1024] = acc_in[:, :1024] + part
            acc[:, 1024:] = acc_in[:, 1024:] + small
        else:
            acc[:, :1024] = part
            acc[:, 1024:] = small

    @pl.when(step == 1)
    def _():
        if last:
            for i in range(8):
                cut = slice(i * LANE, (i + 1) * LANE)
                out_ref[at[i]] = (acc[:, cut] + part[:, cut]).astype(BF16)
            out_ref[8] = (acc[:, 1024:] + small).astype(BF16)
        else:
            out_ref[:, :1024] = acc[:, :1024] + part
            out_ref[:, 1024:] = acc[:, 1024:] + small


def enter_back_kernel(sc, own, other, x_in, dres_in, n_in, gain, down, out_ref, gdown_out):
    step = pl.program_id(0)
    small = (own[8].astype(F32) + other[8].astype(F32)).astype(BF16)
    dnorm = lanes([own[i].astype(F32) + other[i].astype(F32) for i in range(8)]) + dot(small, widen(down[0], LANE))
    hat, scale = center(lanes([x_in[i] for i in range(8)]).astype(F32))
    weighted = dnorm * gain[...].astype(F32)
    first = jnp.mean(weighted, axis=-1, keepdims=True)
    second = jnp.mean(weighted * hat, axis=-1, keepdims=True)
    out_ref[...] = (lanes([dres_in[i] for i in range(8)]) + scale * (weighted - first - hat * second)).astype(BF16)
    gdown = dot(small, lanes([n_in[i] for i in range(8)]), 0, 0)[: down.shape[1]]

    @pl.when(step == 0)
    def _():
        gdown_out[...] = gdown

    @pl.when(step != 0)
    def _():
        gdown_out[...] += gdown


def body(
    x_in,
    out_grad,
    ln1_gain,
    ln1_shift,
    ln2_gain,
    ln2_shift,
    w_qkv,
    qv_bias,
    w_out,
    out_bias,
    w_fc1,
    fc1_bias,
    w_fc2,
    fc2_bias,
    a_qkv,
    b_qkv,
    a_out,
    b_out,
    a_fc1,
    b_fc1,
    a_fc2,
    b_fc2,
    adapter_index,
    valid_tokens,
    live_images,
):
    slots, used, width = x_in.shape
    adapters, rank, _ = b_out.shape
    groups = lax.axis_size("q")
    line = lax.axis_size("tensor")
    q = lax.axis_index("q")
    c = lax.axis_index("c")
    z = lax.axis_index("tensor")
    fast = groups == 4
    quarter = -(-used // 32) * 32
    total = quarter * line
    half_hidden = w_fc1.shape[1] // 2
    half_feat = w_qkv.shape[2] // 2
    swap = [(0, 1), (1, 0)]

    def sibling(value):
        return lax.ppermute(value, "c", swap)

    def by_core(mine, other):
        return jnp.where(c == 0, mine, other), jnp.where(c == 0, other, mine)

    own_info = jnp.concatenate([adapter_index, valid_tokens, live_images, jnp.zeros((3,), jnp.int32)])
    info0, info1 = by_core(own_info, sibling(own_info))
    ads4 = jnp.concatenate([info0[0:2], info1[0:2]])
    lens4 = jnp.concatenate([info0[2:4], info1[2:4]])
    lives = jnp.stack([info0[4], info1[4]])
    ad = ads4[z]
    length = lens4[z]
    live = (z % 2 < lives[z // 2]).astype(jnp.int32)

    parity = z % 2
    to_a = [(cc * 4 + zz, (zz // 2) * 4 + 2 * cc + zz % 2) for cc in range(2) for zz in range(4)]
    to_b = [(cc * 4 + zz, (zz // 2) * 4 + 2 * cc + 1 - zz % 2) for cc in range(2) for zz in range(4)]
    back_a = [(b, a) for a, b in to_a]
    back_b = [(b, a) for a, b in to_b]

    def to_chip(value):
        padded = jnp.pad(value, ((0, 0), (0, quarter - used), (0, 0)))
        first = lax.dynamic_index_in_dim(padded, parity, 0, keepdims=False)
        second = lax.dynamic_index_in_dim(padded, 1 - parity, 0, keepdims=False)
        ra = lax.ppermute(first, ("c", "tensor"), to_a)
        rb = lax.ppermute(second, ("c", "tensor"), to_b)
        return ra, rb, sibling(ra), sibling(rb)

    def from_chip(value):
        own = lax.dynamic_slice_in_dim(value, c * 2 * quarter, 2 * quarter, 0).reshape(2, quarter, width)
        sa = lax.dynamic_index_in_dim(own, parity, 0, keepdims=False)[:used]
        sb = lax.dynamic_index_in_dim(own, 1 - parity, 0, keepdims=False)[:used]
        ra = lax.ppermute(sa, ("c", "tensor"), back_a)
        rb = lax.ppermute(sb, ("c", "tensor"), back_b)
        return jnp.stack([jnp.where(parity == 0, ra, rb), jnp.where(parity == 0, rb, ra)])

    qpos = [2 * c + parity, 2 * c + 1 - parity, 2 * (1 - c) + parity, 2 * (1 - c) + 1 - parity]

    t_qkv = w_qkv.transpose(1, 0, 2)
    aqkv_t = a_qkv.transpose(0, 2, 1)
    afc1_t = a_fc1.transpose(0, 2, 1)
    bqkv_t = b_qkv.transpose(0, 2, 1, 3)
    aout_t = a_out.transpose(0, 2, 1)
    afc2_t = a_fc2.transpose(0, 2, 1)

    def split(value, axis):
        size = value.shape[axis] // 2
        mine = lax.dynamic_slice_in_dim(value, c * size, size, axis)
        other = lax.dynamic_slice_in_dim(value, (1 - c) * size, size, axis)
        return mine, other

    def lane_blocks(value):
        rows, cols = value.shape
        return value.reshape(rows, cols // LANE, LANE).transpose(1, 0, 2)

    small_one = [
        split(bqkv_t, 3)[0][ads4].reshape(4, 3 * rank, LANE),
        split(aout_t, 2)[0][ads4],
    ]
    small_one = jnp.concatenate(small_one, axis=1)
    bias_one = split(qv_bias, 1)[0]
    up_fc1 = split(b_fc1, 2)[0][ads4].reshape(4, rank, half_hidden // LANE, LANE).transpose(0, 2, 1, 3)
    dn_fc2 = split(afc2_t, 2)[0][ads4].reshape(4, rank, half_hidden // LANE, LANE).transpose(0, 2, 1, 3)
    small_two = jnp.concatenate([up_fc1, dn_fc2], axis=1).reshape(4, -1, LANE)
    bias_two = split(fc1_bias.reshape(1, -1), 1)[0].reshape(-1, LANE)
    pad_rows = 16

    def tail_rows(block):
        return jnp.pad(block, ((0, pad_rows - block.shape[0]), (0, 0)))

    extra_one = jnp.concatenate([small_one.reshape(-1, LANE), tail_rows(bias_one)], axis=0)
    extra_two = jnp.concatenate([small_two.reshape(-1, LANE), tail_rows(bias_two)], axis=0)

    if fast:
        m_qkv, o_qkv = split(t_qkv, 2)
        m_out, o_out = split(w_out, 0)
        m_fc1, o_fc1 = split(w_fc1, 1)
        m_fc2, o_fc2 = split(w_fc2, 0)
        mine_one = jnp.concatenate([m_qkv, m_out[None]], axis=0)
        send_one = jnp.concatenate([o_qkv, o_out[None]], axis=0)
        mine_two = jnp.concatenate([lane_blocks(m_fc1), m_fc2.reshape(-1, LANE, LANE)], axis=0)
        send_two = jnp.concatenate([lane_blocks(o_fc1), o_fc2.reshape(-1, LANE, LANE)], axis=0)
        near = [(0, 1), (1, 0), (2, 3), (3, 2)]
        middle = [(1, 2), (2, 1)]
        outer = [(1, 0), (2, 3)]
        xs = [(i, i ^ 1) for i in range(4)]
        ys = [(i, i ^ 2) for i in range(4)]
        at_middle = (z == 1) | (z == 2)

        def gather(mine, send, extra):
            count = mine.shape[0]
            own = jnp.stack([mine, sibling(send)])
            flat = own.reshape(-1, LANE)
            base = flat.shape[0]
            packed = jnp.concatenate([flat, extra], axis=0)
            got1 = lax.ppermute(packed, "tensor", near)
            pair = jnp.stack([packed, got1])
            got2 = lax.ppermute(pair, "tensor", middle)
            got3 = lax.ppermute(got2, "tensor", outer)
            far = jnp.where(at_middle, got2, got3)

            def planes(block):
                one = block[:, :base].reshape(2, 2, count, LANE, LANE)
                gx = lax.ppermute(one, "q", xs)
                gy = lax.ppermute(one, "q", ys)
                da = lax.ppermute(gy[0:1], "q", xs)
                db = lax.ppermute(gx[1:2], "q", ys)
                return (one, gx, gy, da, db)

            extras = jnp.concatenate([pair[:, base:], far[:, base:]], axis=0)
            return planes(pair), planes(far), extras

        first_a, first_b, extras_one = gather(mine_one, send_one, extra_one)
        second_a, second_b, extras_two = gather(mine_two, send_two, extra_two)
        tmap = [z, z ^ 1, jnp.where(z < 2, 2, 1), jnp.where(z < 2, 3, 0)]
        idx = [2 * (q ^ j) + (c ^ k) for j in range(4) for k in range(2)]
    else:
        def everywhere(value, axis):
            return lax.all_gather(lax.all_gather(value, ("q", "c"), axis=axis, tiled=True), "tensor", axis=0)

        g_qkv = split(everywhere(t_qkv, 1), 3)[0]
        g_out = split(everywhere(w_out, 1), 1)[0]
        g_fc1 = split(everywhere(w_fc1, 0), 2)[0]
        g_fc2 = split(everywhere(w_fc2, 1), 1)[0]
        lb = half_hidden // LANE
        one = jnp.concatenate(
            [
                g_qkv.reshape(4, 3, 4, 2, LANE, LANE).transpose(2, 0, 3, 1, 4, 5),
                g_out.reshape(4, 1, LANE, 4, 2, LANE).transpose(3, 0, 4, 1, 2, 5),
            ],
            axis=3,
        )
        two = jnp.concatenate(
            [
                g_fc1.reshape(4, 4, 2, LANE, lb, LANE).transpose(1, 0, 2, 4, 3, 5),
                g_fc2.reshape(4, lb, LANE, 4, 2, LANE).transpose(3, 0, 4, 1, 2, 5),
            ],
            axis=3,
        )

        def planes(value, at):
            return (value[0, at : at + 2], value[1, at : at + 2], value[2, at : at + 2], value[3, at : at + 1], value[3, at + 1 : at + 2])

        first_a, first_b = planes(one, 0), planes(one, 2)
        second_a, second_b = planes(two, 0), planes(two, 2)
        extras_one = lax.all_gather(extra_one, "tensor", axis=0)
        extras_two = lax.all_gather(extra_two, "tensor", axis=0)
        tmap = [jnp.int32(0) + n for n in range(4)]
        idx = [jnp.int32(0) + n for n in range(8)]

    def of_image(block, at, count):
        part = block[:, at : at + 4 * count].reshape(4, 4, count, LANE)
        return lax.dynamic_index_in_dim(part, z, 1, keepdims=False)

    picked_one = of_image(extras_one, 0, 4 * rank)
    up_qkv = picked_one[:, : 3 * rank].reshape(4, 3, rank, LANE)
    down_out = picked_one[:, 3 * rank :]
    bias_qv = extras_one[:, 16 * rank : 16 * rank + 2]
    lb = half_hidden // LANE
    picked_two = of_image(extras_two, 0, 2 * lb * rank).reshape(4, 2, lb, rank, LANE)
    up_one = picked_two[:, 0]
    down_two = picked_two[:, 1]
    bias_fc1 = extras_two[:, 8 * lb * rank : 8 * lb * rank + lb]

    values = [ad, length, live, c, z, 0, 0, 0] + idx + tmap + qpos
    sc = jnp.stack([jnp.asarray(v, jnp.int32) for v in values])

    row = lambda v: v.reshape(1, -1)
    by_adapter = lambda v: pl.BlockSpec((1,) + v.shape[1:], lambda i, s: (s[AD], 0, 0))
    chunked = jax.ShapeDtypeStruct((8, total, LANE), BF16)
    chunked_wide = jax.ShapeDtypeStruct((8, total, LANE), F32)
    nine = jax.ShapeDtypeStruct((9, total, LANE), BF16)
    narrow = jax.ShapeDtypeStruct((total, LANE), BF16)
    acc_wide = jax.ShapeDtypeStruct((total, width + LANE), F32)

    xq = to_chip(x_in)
    x_c, n1_c, uq = call(
        functools.partial(enter_kernel, 8),
        sc,
        (*xq, row(ln1_gain), row(ln1_shift), aqkv_t),
        [full((quarter, width))] * 4 + [full((1, width))] * 2 + [by_adapter(aqkv_t)],
        [full((8, total, LANE)), full((8, total, LANE)), full((total, LANE))],
        [chunked, chunked, narrow],
        (1,),
        name="enter",
    )
    gq = to_chip(out_grad)
    d_c, du2 = call(
        cotangent_kernel,
        sc,
        (*gq, b_fc2),
        [full((quarter, width))] * 4 + [by_adapter(b_fc2)],
        [full((8, total, LANE)), full((total, LANE))],
        [chunked, narrow],
        (1,),
        name="cotangent",
    )

    def plane_specs(planes):
        tail = planes[0].shape[1:]
        stepped = pl.BlockSpec((1,) + tail, lambda t, s: (t,) + (0,) * len(tail))
        return [stepped] * 3 + [full((1,) + tail)] * 2

    def stepped(value, base):
        tail = value.shape[1:]
        return pl.BlockSpec((1,) + tail, lambda t, s: (base + t,) + (0,) * len(tail))

    def step_out(tail):
        return pl.BlockSpec((1,) + tail, lambda t, s: (t,) + (0,) * len(tail))

    acc_spec = full((total, width + LANE))

    def attend(planes, base, acc):
        last = acc is not None
        held = pltpu.VMEM((1,) + planes[0].shape[1:], BF16)
        return call(
            functools.partial(attend_kernel, used, last),
            sc,
            (n1_c, uq, *planes, up_qkv, bias_qv, down_out) + ((acc,) if last else ()),
            [full((8, total, LANE)), full((total, LANE))]
            + plane_specs(planes)
            + [stepped(up_qkv, base), stepped(bias_qv, base), stepped(down_out, base)]
            + ([acc_spec] if last else []),
            [
                step_out((3, total, LANE)),
                step_out((total, LANE)),
                step_out((8, total)),
                full((9, total, LANE)) if last else acc_spec,
            ],
            [
                jax.ShapeDtypeStruct((2, 3, total, LANE), BF16),
                jax.ShapeDtypeStruct((2, total, LANE), BF16),
                jax.ShapeDtypeStruct((2, 8, total), F32),
                nine if last else acc_wide,
            ],
            (2,),
            scratch=(held, pltpu.VMEM((total, width + LANE), F32)),
            name="attend",
            cost=(4 << 30, 8 << 20),
        )

    qkv_a, o_a, lse_a, acc_one = attend(first_a, 0, None)
    qkv_b, o_b, lse_b, branch = attend(first_b, 2, acc_one)
    branch_other = sibling(branch)

    per_row = total // quarter
    chunk_rows = pl.BlockSpec((8, quarter, LANE), lambda i, s: (0, i, 0))
    nine_rows = pl.BlockSpec((9, quarter, LANE), lambda i, s: (0, i, 0))
    narrow_rows = pl.BlockSpec((quarter, LANE), lambda i, s: (i, 0))
    resid, n2_c, u1, uo = call(
        middle_kernel,
        sc,
        (branch, branch_other, x_c, row(out_bias), b_out, row(ln2_gain), row(ln2_shift), afc1_t),
        [nine_rows, nine_rows, chunk_rows, full((1, width)), by_adapter(b_out), full((1, width)), full((1, width)), by_adapter(afc1_t)],
        [chunk_rows, chunk_rows, narrow_rows, narrow_rows],
        [chunked_wide, chunked, narrow, narrow],
        (per_row,),
        name="middle",
    )

    def feed(planes, base, accs):
        last = accs is not None
        held = pltpu.VMEM((1,) + planes[0].shape[1:], BF16)
        out = [nine, nine] if last else [acc_wide, acc_wide]
        out_spec = [full((9, total, LANE))] * 2 if last else [acc_spec] * 2
        return call(
            functools.partial(feed_kernel, last),
            sc,
            (n2_c, u1, d_c, du2, *planes, up_one, down_two, bias_fc1) + (tuple(accs) if last else ()),
            [full((8, total, LANE)), full((total, LANE)), full((8, total, LANE)), full((total, LANE))]
            + plane_specs(planes)
            + [stepped(up_one, base), stepped(down_two, base), stepped(bias_fc1, base)]
            + ([acc_spec] * 2 if last else []),
            out_spec + [step_out((lb, rank, LANE))] * 2,
            out + [jax.ShapeDtypeStruct((2, lb, rank, LANE), BF16)] * 2,
            (2,),
            scratch=(
                held,
                pltpu.VMEM((total, width + LANE), F32),
                pltpu.VMEM((total, width + LANE), F32),
                pltpu.VMEM((total, half_hidden), BF16),
                pltpu.VMEM((total, half_hidden), BF16),
            ),
            name="feed",
            cost=(6 << 30, 12 << 20),
        )

    y_one, dn_one, gb1_a, ga2_a = feed(second_a, 0, None)
    y_all, dn_all, gb1_b, ga2_b = feed(second_b, 2, (y_one, dn_one))
    dn_other = sibling(dn_all)
    y_other = sibling(y_all)

    dres, dz_c, duo, g_afc1, g_bout = call(
        middle_back_kernel,
        sc,
        (dn_all, dn_other, resid, d_c, n2_c, uo, row(ln2_gain), afc1_t, b_out),
        [nine_rows, nine_rows, chunk_rows, chunk_rows, chunk_rows, narrow_rows, full((1, width)), by_adapter(afc1_t), by_adapter(b_out)],
        [chunk_rows, chunk_rows, narrow_rows, full((rank, width)), full((rank, width))],
        [chunked_wide, chunked, narrow] + [jax.ShapeDtypeStruct((rank, width), F32)] * 2,
        (per_row,),
        name="middle_back",
    )
    out_rows, g_bfc2 = call(
        leave_kernel,
        sc,
        (y_all, y_other, resid, row(fc2_bias), b_fc2, d_c),
        [nine_rows, nine_rows, chunk_rows, full((1, width)), by_adapter(b_fc2), chunk_rows],
        [pl.BlockSpec((quarter, width), lambda i, s: (i, 0)), full((rank, width))],
        [jax.ShapeDtypeStruct((total, width), BF16), jax.ShapeDtypeStruct((rank, width), F32)],
        (per_row,),
        name="leave",
    )
    layer_out = from_chip(out_rows)

    def attend_back(planes, base, qkv, o, lse, acc):
        last = acc is not None
        held = pltpu.VMEM((1,) + planes[0].shape[1:], BF16)
        return call(
            functools.partial(attend_back_kernel, used, last),
            sc,
            (dz_c, duo, uq, qkv, o, lse, *planes, up_qkv, down_out) + ((acc,) if last else ()),
            [full((8, total, LANE)), full((total, LANE)), full((total, LANE))]
            + [step_out((3, total, LANE)), step_out((total, LANE)), step_out((8, total))]
            + plane_specs(planes)
            + [stepped(up_qkv, base), stepped(down_out, base)]
            + ([acc_spec] if last else []),
            [full((9, total, LANE)) if last else acc_spec, step_out((3, rank, LANE)), step_out((rank, LANE))],
            [
                nine if last else acc_wide,
                jax.ShapeDtypeStruct((2, 3, rank, LANE), BF16),
                jax.ShapeDtypeStruct((2, rank, LANE), BF16),
            ],
            (2,),
            scratch=(held, pltpu.VMEM((total, width + LANE), F32), pltpu.VMEM((total, LANE), BF16)),
            name="attend_back",
            cost=(6 << 30, 8 << 20),
        )

    dn1_one, gbq_a, gao_a = attend_back(first_a, 0, qkv_a, o_a, lse_a, None)
    dn1_all, gbq_b, gao_b = attend_back(first_b, 2, qkv_b, o_b, lse_b, dn1_one)
    dn1_other = sibling(dn1_all)
    grad_rows, g_aqkv = call(
        enter_back_kernel,
        sc,
        (dn1_all, dn1_other, x_c, dres, n1_c, row(ln1_gain), aqkv_t),
        [nine_rows, nine_rows, chunk_rows, chunk_rows, chunk_rows, full((1, width)), by_adapter(aqkv_t)],
        [pl.BlockSpec((quarter, width), lambda i, s: (i, 0)), full((3 * rank, width))],
        [jax.ShapeDtypeStruct((total, width), BF16), jax.ShapeDtypeStruct((3 * rank, width), F32)],
        (per_row,),
        name="enter_back",
    )
    x_grad = from_chip(grad_rows)

    t_order = jnp.stack([jnp.asarray(v, jnp.int32) for v in tmap])

    def canonical(a, b):
        joined = jnp.concatenate([a, b], axis=0)
        where = jnp.argmax(t_order[None, :] == jnp.arange(4)[:, None], axis=1)
        return joined[where]

    def half_of(value):
        part = lax.dynamic_slice_in_dim(value, c * (width // 2), width // 2, 1)
        return part.reshape(value.shape[0], -1, LANE).astype(BF16)

    def exchange(sharded, shared):
        if fast:
            def packed(step):
                block = lax.dynamic_index_in_dim(sharded, (z + step) % 4, 0, keepdims=False)
                return jnp.concatenate([block, shared], axis=0)

            got = [packed(0)] + [
                lax.ppermute(packed(n), "tensor", [(i, (i + n) % 4) for i in range(4)]) for n in range(1, 4)
            ]
            block = jnp.stack(got)
            others = [lax.ppermute(block, "q", [(i, i ^ n) for i in range(4)]) for n in range(1, 4)]
            return jnp.concatenate([block] + others, axis=0)
        packed = jnp.concatenate([sharded.reshape(-1, LANE), shared], axis=0)
        everything = lax.all_gather(packed, ("q", "tensor"), axis=0)
        rows = sharded.shape[1]
        part = everything[:, : 4 * rows].reshape(-1, 4, rows, LANE)
        return jnp.concatenate(
            [lax.dynamic_index_in_dim(part, z, 1, keepdims=False), everything[:, 4 * rows :]], axis=1
        )

    ident = jnp.full((16, LANE), ad, jnp.int32).astype(BF16)
    g_aout = canonical(gao_a, gao_b)
    early_sharded = jnp.concatenate(
        [
            canonical(gb1_a, gb1_b).reshape(4, -1, LANE),
            canonical(ga2_a, ga2_b).reshape(4, -1, LANE),
        ],
        axis=1,
    )
    early_shared = jnp.concatenate(
        [half_of(g_bout).reshape(-1, LANE), half_of(g_afc1).reshape(-1, LANE), half_of(g_bfc2).reshape(-1, LANE), ident],
        axis=0,
    )
    late_sharded = jnp.concatenate([canonical(gbq_a, gbq_b).reshape(4, -1, LANE), g_aout], axis=1)
    late_shared = half_of(g_aqkv).reshape(-1, LANE)
    early = exchange(early_sharded, early_shared)
    late = exchange(late_sharded, late_shared)
    images = early.shape[0]
    names = early[:, -1, 0].astype(F32)
    onehot = (names[None, :] == jnp.arange(adapters, dtype=F32)[:, None]).astype(BF16)

    def table(value):
        return jnp.einsum("ni,irl->nrl", onehot, value, preferred_element_type=F32)

    early_sum = table(early[:, :-16])
    late_sum = table(late)
    early0, early1 = by_core(early_sum, sibling(early_sum))
    late0, late1 = by_core(late_sum, sibling(late_sum))
    both_early = jnp.stack([early0, early1])
    both_late = jnp.stack([late0, late1])

    def hidden_like(value):
        return value.reshape(2, adapters, lb, rank, LANE).transpose(1, 3, 0, 2, 4).reshape(adapters, rank, -1)

    def wide_like(value, count):
        return value.reshape(2, adapters, count, 4, LANE).transpose(1, 2, 0, 3, 4).reshape(adapters, count, width)

    edge = lb * rank
    grad_b_fc1 = hidden_like(both_early[:, :, :edge])
    grad_a_fc2 = hidden_like(both_early[:, :, edge : 2 * edge]).transpose(0, 2, 1)
    at = 2 * edge
    grad_b_out = wide_like(both_early[:, :, at : at + 4 * rank], rank)
    grad_a_fc1 = wide_like(both_early[:, :, at + 4 * rank : at + 8 * rank], rank).transpose(0, 2, 1)
    grad_b_fc2 = wide_like(both_early[:, :, at + 8 * rank : at + 12 * rank], rank)
    qkv_part = both_late[:, :, : 3 * rank].reshape(2, adapters, 3, rank, LANE)
    grad_b_qkv = qkv_part.transpose(1, 3, 2, 0, 4).reshape(adapters, rank, 3, 2 * LANE)
    grad_a_out = both_late[:, :, 3 * rank : 4 * rank].transpose(1, 2, 0, 3).reshape(adapters, rank, 2 * LANE).transpose(0, 2, 1)
    grad_a_qkv = wide_like(both_late[:, :, 4 * rank :], 3 * rank).transpose(0, 2, 1)
    return (
        layer_out,
        x_grad,
        grad_a_qkv,
        grad_b_qkv,
        grad_a_out,
        grad_b_out,
        grad_a_fc1,
        grad_b_fc1,
        grad_a_fc2,
        grad_b_fc2,
    )


def solution(mesh):
    devices = np.asarray(mesh.devices)
    rows, line = devices.shape
    cut = Mesh(devices.reshape(rows // 2, 2, line), ("q", "c", "tensor"))
    dp = ("q", "c")
    placed = (
        P(dp, "tensor", None),
        P(dp, "tensor", None),
        P(),
        P(),
        P(),
        P(),
        P(dp, None, "tensor"),
        P(None, "tensor"),
        P("tensor", dp),
        P(),
        P(dp, "tensor"),
        P("tensor"),
        P("tensor", dp),
        P(),
        P(),
        P(None, None, None, "tensor"),
        P(None, "tensor", None),
        P(),
        P(),
        P(None, None, "tensor"),
        P(None, "tensor", None),
        P(),
        P(dp),
        P(dp),
        P(dp),
    )
    return jax.shard_map(
        body,
        mesh=cut,
        in_specs=placed,
        out_specs=(
            P(dp, "tensor", None),
            P(dp, "tensor", None),
            P(),
            P(None, None, None, "tensor"),
            P(None, "tensor", None),
            P(),
            P(),
            P(None, None, "tensor"),
            P(None, "tensor", None),
            P(),
        ),
        check_vma=False,
    )
```
